32 devices in a mesh: tm: 4 (over y, x), feat: 8 (over z, core).
Axes of the slice: x: 2, y: 2, z: 4, core: 2. Of those that a mesh axis runs over, the one named last changes fastest.
Arguments:
- dictionary: bfloat16 [8192, 16384], P('tm', 'feat'), may hold values from -6 to 6
- eigvecs: bfloat16 [16384, 256], P('feat'), may hold values from -0.046875 to 0.046875
- snapshots: float32 [16384, 8192], P('feat', 'tm'), may hold values from -0.0625 to 0.0625
Outputs:
- modes: float32 [16384, 256], P(('feat', 'tm'))
The draws below stay inside these ranges and needn't reach their ends.
All inputs are finite; a program needn't handle non-finite values.
Results may differ from the reference program's by a relative error of at most 0.0003.
Values sent between devices are 32-bit elements; how exact they have to be, the bound alone decides.
No kernel may reach another device: no remote copies, remote signals or barrier semaphores. Data moves between devices by JAX's collectives and lax.ppermute only.
A program may use at most 64 MiB of HBM per device.

```python
import jax
import jax.numpy as jnp
from jax import lax

FUNCS = 16384
MODES = 256
SNAPS = 8192
CELLS = 16384


def level_of(rng, shape, pieces, least, top_value):
    gain = 1.0
    for axis_at, blocks in pieces:
        heights = jax.random.uniform(jax.random.fold_in(jax.random.fold_in(rng, 6), axis_at), (blocks,), jnp.float32, least / len(pieces), top_value / len(pieces))
        gain = gain * jnp.repeat(jnp.exp(heights), shape[axis_at] // blocks).reshape((-1,) + (1,) * (len(shape) - 1 - axis_at))
    return gain


def centred(stream_key, dims, width, limit, pieces=(), held_as=jnp.bfloat16):
    values = width * jax.random.normal(stream_key, dims, jnp.float32)
    if pieces:
        values = values * level_of(stream_key, dims, pieces, -0.22, 0.18)
    return jnp.clip(values, -limit, limit).astype(held_as)


def setup_inputs(seed: int = 0) -> dict:
    keys = jax.random.split(jax.random.key(seed), 4)
    dictionary = centred(keys[0], (SNAPS, FUNCS), 1.0, 6.0, ((0, 4), (1, 8)))
    eigvecs = centred(keys[1], (FUNCS, MODES), FUNCS ** -0.5, 0.046875, ((0, 8),))
    snapshots = centred(keys[2], (CELLS, SNAPS), SNAPS ** -0.5, 0.0625, ((0, 8), (1, 4)), jnp.float32)
    return dict(dictionary=dictionary, eigvecs=eigvecs, snapshots=snapshots)


def reference(dictionary, eigvecs, snapshots):
    coefficients = jnp.dot(dictionary, eigvecs, preferred_element_type=jnp.float32)
    return jnp.dot(snapshots, coefficients, precision=lax.Precision.HIGHEST, preferred_element_type=jnp.float32)
```

```python
import functools

import jax
import jax.numpy as jnp
from jax import lax
from jax.experimental import pallas as pl
from jax.experimental.pallas import tpu as pltpu
from jax.sharding import PartitionSpec as P

PARTS = 2
F32, BF16 = jnp.float32, jnp.bfloat16


def swap(x, axis, size, bit):
    return lax.ppermute(x, axis, [(i, i ^ bit) for i in range(size)])


def halves(x):
    hi = x.astype(BF16)
    return hi, (x - hi.astype(F32)).astype(BF16)


def project_kernel(ids, d_ref, e_ref, o_ref):
    o_ref[0] = jnp.dot(d_ref[...], e_ref[...], preferred_element_type=F32)


def project(dictionary, eigvecs, ids, rows):
    depth, modes = eigvecs.shape
    n = ids.shape[0]
    return pl.pallas_call(
        project_kernel,
        grid_spec=pltpu.PrefetchScalarGridSpec(
            num_scalar_prefetch=1,
            grid=(n,),
            in_specs=[
                pl.BlockSpec((rows, depth), lambda i, ids: (ids[i], 0)),
                pl.BlockSpec(memory_space=pltpu.VMEM),
            ],
            out_specs=pl.BlockSpec((1, rows, modes), lambda i, ids: (i, 0, 0)),
        ),
        out_shape=jax.ShapeDtypeStruct((n, rows, modes), F32),
        compiler_params=pltpu.CompilerParams(vmem_limit_bytes=12 << 20),
        cost_estimate=pl.CostEstimate(
            flops=2 * n * rows * depth * modes,
            bytes_accessed=2 * n * rows * depth,
            transcendentals=0,
        ),
        name="project",
    )(
        ids,
        pltpu.with_memory_space_constraint(dictionary, pltpu.HBM),
        pltpu.with_memory_space_constraint(eigvecs, pltpu.VMEM),
    )


def split_kernel(ids, s_ref, hi_ref, lo_ref):
    step = s_ref.shape[0]
    rows = pl.ds(pl.multiple_of(pl.program_id(0) * step, step), step)
    hi_ref[rows, :], lo_ref[rows, :] = halves(s_ref[...])


def split(snapshots, block, rows, step=128):
    width = snapshots.shape[1]
    n = rows // step
    return pl.pallas_call(
        split_kernel,
        grid_spec=pltpu.PrefetchScalarGridSpec(
            num_scalar_prefetch=1,
            grid=(n,),
            in_specs=[pl.BlockSpec((step, width), lambda i, b: (b[0] * n + i, 0))],
            out_specs=[pl.BlockSpec(memory_space=pltpu.VMEM)] * 2,
        ),
        out_shape=[pltpu.VMEM((rows, width), BF16)] * 2,
        compiler_params=pltpu.CompilerParams(vmem_limit_bytes=8 << 20),
        cost_estimate=pl.CostEstimate(
            flops=0, bytes_accessed=4 * rows * width, transcendentals=0
        ),
        name="split",
    )(block[None], pltpu.with_memory_space_constraint(snapshots, pltpu.HBM))


def order(bits):
    if not bits:
        return [0]
    rest = order(bits[1:])
    return [m | bits[0] for m in rest] + rest


def reconstruct_kernel(n, orders, n_acc, ids, *refs):
    his, los = refs[:n], refs[n : 2 * n]
    n_c = len(refs) - 2 * n - n_acc - 5
    cs = refs[2 * n : 2 * n + n_c]
    accs = refs[2 * n + n_c : 2 * n + n_c + n_acc]
    outs, both = refs[-5:-1], refs[-1]
    rows, cols = cs[0].shape[-2:]
    k = 0
    for c in cs:
        for j in range(c.shape[0]):
            hi, lo = halves(c[j])
            both[k * rows : (k + 1) * rows, :cols] = hi
            both[k * rows : (k + 1) * rows, cols:] = lo
            k += 1
    tall = his[0].shape[0] // 2
    for p, masks in enumerate(orders):
        for at, mask in enumerate(masks):
            total = None
            for j in range(k):
                where = (
                    slice(p * tall, (p + 1) * tall),
                    pl.ds(pl.multiple_of(ids[j] * rows, rows), rows),
                )
                c = both[j * rows : (j + 1) * rows, :]
                wide = jnp.dot(his[mask][where], c, preferred_element_type=F32)
                low = jnp.dot(los[mask][where], c[:, :cols], preferred_element_type=F32)
                term = (wide[:, cols:] + low) + wide[:, :cols]
                total = term if total is None else total + term
            out = 2 * p + at // (n // 2)
            place = at % (n // 2)
            if n_acc:
                total = total + accs[out][place]
            outs[out][place] = total


def reconstruct(split_rows, cs, ids, orders, accs):
    n = len(split_rows)
    his, los = [hi for hi, _ in split_rows], [lo for _, lo in split_rows]
    rows, cols = cs[0].shape[-2:]
    depth = rows * sum(c.shape[0] for c in cs)
    tall = his[0].shape[0] // 2
    vmem = pl.BlockSpec(memory_space=pltpu.VMEM)
    n_in = 2 * n + len(cs)
    ins = [pltpu.with_memory_space_constraint(x, pltpu.VMEM) for x in (*his, *los, *cs, *accs)]
    return pl.pallas_call(
        functools.partial(reconstruct_kernel, n, orders, len(accs)),
        grid_spec=pltpu.PrefetchScalarGridSpec(
            num_scalar_prefetch=1,
            grid=(),
            in_specs=[vmem] * len(ins),
            out_specs=[vmem] * 4,
            scratch_shapes=[pltpu.VMEM((depth, 2 * cols), BF16)],
        ),
        out_shape=[pltpu.VMEM((n // 2, tall, cols), F32)] * 4,
        input_output_aliases={1 + n_in + i: i for i in range(len(accs))},
        compiler_params=pltpu.CompilerParams(vmem_limit_bytes=8 << 20),
        cost_estimate=pl.CostEstimate(
            flops=8 * n * tall * depth * cols * 2, bytes_accessed=0, transcendentals=0
        ),
        name="reconstruct",
    )(ids, *ins)


def shards(n_feat, n_tm, dictionary, eigvecs, snapshots):
    feat, tm = lax.axis_index("feat"), lax.axis_index("tm")
    snaps, modes = dictionary.shape[0], eigvecs.shape[1]
    core, pair = feat & 1, (feat >> 1) & 1
    rows = snaps // (4 * PARTS)
    cols = modes // 2
    cells = snapshots.shape[0] // n_tm

    def block(part, other_core, other_pair):
        return (((core ^ other_core) * PARTS + part) * 2 + (pair ^ other_pair)).astype(jnp.int32)

    sums = []
    for part in range(PARTS):
        theirs = project(dictionary, eigvecs, jnp.stack([block(part, 1, 1), block(part, 1, 0)]), rows)
        theirs = swap(theirs, "feat", n_feat, 1)
        mine = project(dictionary, eigvecs, jnp.stack([block(part, 0, 1), block(part, 0, 0)]), rows)
        sums.append((mine, theirs))

    split_rows = [split(snapshots, (tm ^ mask).astype(jnp.int32), cells) for mask in range(n_tm)]

    tm_bits = [1 << i for i in range(n_tm.bit_length() - 1)]
    bit_orders = (tm_bits, tm_bits[::-1])
    orders = [order(bits) for bits in bit_orders]
    done = []
    for half in range(2):
        at = slice(half * cols, (half + 1) * cols)
        accs = []
        for part, (mine, theirs) in enumerate(sums):
            total = swap(mine[0, :, at] + theirs[0, :, at], "feat", n_feat, 2)
            total = total + (mine[1, :, at] + theirs[1, :, at])
            bit = 4
            while bit < n_feat:
                total = total + swap(total, "feat", n_feat, bit)
                bit *= 2
            own = jnp.stack([swap(total, "feat", n_feat, 2), total])
            other = swap(own, "feat", n_feat, 1)
            ids = jnp.stack([block(part, dc, dp) for dc in (1, 0) for dp in (1, 0)])
            accs = reconstruct(split_rows, [other, own], ids, orders, accs)
        results = []
        for p, bits in enumerate(bit_orders):
            send, keep = accs[2 * p], accs[2 * p + 1]
            for bit in bits:
                keep = keep + swap(send, "tm", n_tm, bit)
                n = keep.shape[0] // 2
                send, keep = keep[:n], keep[n:] if n else keep
            results.append(keep[0])
        done.append(jnp.concatenate(results, 0))
    return jnp.concatenate(done, 1)


def solution(mesh):
    n_feat, n_tm = mesh.shape["feat"], mesh.shape["tm"]
    return jax.shard_map(
        functools.partial(shards, n_feat, n_tm),
        mesh=mesh,
        in_specs=(P("tm", "feat"), P("feat", None), P("feat", "tm")),
        out_specs=P(("feat", "tm"), None),
        check_vma=False,
    )
```

```python
import functools

import jax
import jax.numpy as jnp
from jax import lax
from jax.experimental import pallas as pl
from jax.experimental.pallas import tpu as pltpu
from jax.sharding import PartitionSpec as P

PARTS = 2
F32, BF16 = jnp.float32, jnp.bfloat16
VMEM = pl.BlockSpec(memory_space=pltpu.VMEM)


def after(x, *earlier):
    return lax.optimization_barrier((x, *earlier))[0]


def swap(x, axis, size, bit):
    return lax.ppermute(x, axis, [(i, i ^ bit) for i in range(size)])


def halves(x):
    hi = x.astype(BF16)
    return hi, (x - hi.astype(F32)).astype(BF16)


def project_kernel(part, ids, d_ref, e_ref, *refs):
    theirs, mine, blocks, sems = refs[:4]
    n, rows, _ = blocks.shape
    copies = []
    if len(refs) > 4:
        e_copy = pltpu.make_async_copy(e_ref, refs[4], refs[5])
        e_copy.start()
        e_ref = refs[4]
    for i in range(n):
        at = pl.ds(pl.multiple_of(ids[1 + part * n + i] * rows, rows), rows)
        copies.append(pltpu.make_async_copy(d_ref.at[at, :], blocks.at[i], sems.at[i]))
        copies[i].start()
    if len(refs) > 4:
        e_copy.wait()
    for i in range(n):
        copies[i].wait()
        out = (theirs, mine)[i // (n // 2)]
        out[i % (n // 2)] = jnp.dot(blocks[i], e_ref[...], preferred_element_type=F32)


def project(dictionary, eigvecs, ids, part, rows):
    depth, modes = eigvecs.shape
    n, first = 4, part == 0
    own = [pltpu.VMEM((depth, modes), BF16), pltpu.SemaphoreType.DMA] if first else []
    hbm = pl.BlockSpec(memory_space=pl.ANY)
    return pl.pallas_call(
        functools.partial(project_kernel, part),
        in_specs=[pl.BlockSpec(memory_space=pltpu.SMEM), hbm, hbm if first else VMEM],
        out_specs=[VMEM] * 2,
        out_shape=[pltpu.VMEM((n // 2, rows, modes), F32)] * 2,
        scratch_shapes=[
            pltpu.VMEM((n, rows, depth), BF16),
            pltpu.SemaphoreType.DMA((n,)),
            *own,
        ],
        compiler_params=pltpu.CompilerParams(vmem_limit_bytes=46 << 20),
        cost_estimate=pl.CostEstimate(
            flops=2 * n * rows * depth * modes,
            bytes_accessed=2 * n * rows * depth,
            transcendentals=0,
        ),
        name="project",
    )(
        ids,
        pltpu.with_memory_space_constraint(dictionary, pltpu.HBM),
        pltpu.with_memory_space_constraint(eigvecs, pltpu.HBM if first else pltpu.VMEM),
    )


def order(bits):
    if not bits:
        return [0]
    rest = order(bits[1:])
    return [m | bits[0] for m in rest] + rest


def reconstruct_kernel(groups, n_c, n_acc, cells, part, ids, s_ref, *refs):
    cs, accs = refs[:n_c], refs[n_c : n_c + n_acc]
    outs, both = refs[n_c + n_acc : -1], refs[-1]
    rows, cols = cs[0].shape[-2:]
    k = 0
    for c in cs:
        for j in range(c.shape[0]):
            hi, lo = halves(c[j])
            both[k * rows : (k + 1) * rows, :cols] = hi
            both[k * rows : (k + 1) * rows, cols:] = lo
            k += 1
    tall = cells // 2
    me = ids[0]
    for g, (p, masks) in enumerate(groups):
        for at, mask in enumerate(masks):
            row = pl.ds(pl.multiple_of((me ^ mask) * cells + p * tall, tall), tall)
            total = accs[g][at] if n_acc else None
            for j in range(k):
                col = pl.ds(pl.multiple_of(ids[1 + part * k + j] * rows, rows), rows)
                hi, lo = halves(s_ref[row, col])
                c = both[j * rows : (j + 1) * rows, :]
                wide = jnp.dot(hi, c, preferred_element_type=F32)
                low = jnp.dot(lo, c[:, :cols], preferred_element_type=F32)
                term = (wide[:, cols:] + low) + wide[:, :cols]
                total = term if total is None else total + term
            outs[g][at] = total


def reconstruct(snapshots, cs, ids, part, groups, cells, accs):
    rows, cols = cs[0].shape[-2:]
    depth = rows * sum(c.shape[0] for c in cs)
    tall = cells // 2
    ins = [pltpu.with_memory_space_constraint(x, pltpu.VMEM) for x in (*cs, *accs)]
    blocks = sum(len(masks) for _, masks in groups)
    return pl.pallas_call(
        functools.partial(reconstruct_kernel, groups, len(cs), len(accs), cells, part),
        in_specs=[pl.BlockSpec(memory_space=pltpu.SMEM)] + [VMEM] * (1 + len(ins)),
        out_specs=[VMEM] * len(groups),
        scratch_shapes=[pltpu.VMEM((depth, 2 * cols), BF16)],
        out_shape=[pltpu.VMEM((len(masks), tall, cols), F32) for _, masks in groups],
        input_output_aliases={2 + len(cs) + i: i for i in range(len(accs))},
        compiler_params=pltpu.CompilerParams(vmem_limit_bytes=8 << 20),
        cost_estimate=pl.CostEstimate(
            flops=8 * blocks * tall * depth * cols, bytes_accessed=0, transcendentals=0
        ),
        name="reconstruct",
    )(ids, snapshots, *ins)


def shards(n_feat, n_tm, dictionary, eigvecs, snapshots):
    feat, tm = lax.axis_index("feat"), lax.axis_index("tm")
    snaps, modes = dictionary.shape[0], eigvecs.shape[1]
    core, pair = feat & 1, (feat >> 1) & 1
    rows = snaps // (4 * PARTS)
    cols = modes // 2
    cells = snapshots.shape[0] // n_tm

    ids = [tm] + [
        ((core ^ dc) * PARTS + part) * 2 + (pair ^ dp)
        for part in range(PARTS)
        for dc in (1, 0)
        for dp in (1, 0)
    ]
    ids = jnp.stack(ids).astype(jnp.int32)

    sums = []
    for part in range(PARTS):
        theirs, mine = project(dictionary, eigvecs, ids, part, rows)
        ids = after(ids, mine)
        theirs = swap(theirs, "feat", n_feat, 1)
        sums.append(mine + theirs)
    snapshots = pltpu.with_memory_space_constraint(after(snapshots, mine), pltpu.VMEM)

    streams = [(half, part) for half in range(2) for part in range(PARTS)]
    lag = 2
    came, full, whole = [], [], []
    for i, (half, part) in enumerate(streams):
        send, keep = (sums[part][j, :, half * cols : (half + 1) * cols] for j in range(2))
        if i >= lag:
            send = after(send, came[i - lag])
        came.append(swap(send, "feat", n_feat, 2))
        total = keep + came[i]
        bit = 4
        while bit < n_feat:
            if i >= lag:
                total = after(total, full[i - lag])
            got = swap(total, "feat", n_feat, bit)
            total = total + got
            bit *= 2
        full.append(got)
        own = jnp.stack([swap(total, "feat", n_feat, 2), total])
        whole.append([swap(own, "feat", n_feat, 1), own])

    tm_bits = [1 << i for i in range(n_tm.bit_length() - 1)]
    bit_orders = (tm_bits, tm_bits[::-1])
    sends, keeps = [], []
    for p, bits in enumerate(bit_orders):
        masks = order(bits)
        sends.append((p, masks[: n_tm // 2]))
        keeps.append((p, masks[n_tm // 2 :]))
    done = []
    for half in range(2):
        accs = []
        for part in range(PARTS):
            cs = whole[half * PARTS + part]
            if half == 1 and part == PARTS - 1:
                send = reconstruct(snapshots, cs, ids, part, sends, cells, accs[:2])
                keep = reconstruct(snapshots, cs, ids, part, keeps, cells, accs[2:])
                accs = send + keep
            else:
                accs = reconstruct(snapshots, cs, ids, part, sends + keeps, cells, accs)
        results = []
        for p, bits in enumerate(bit_orders):
            send, keep = accs[p], accs[2 + p]
            for bit in bits:
                keep = keep + swap(send, "tm", n_tm, bit)
                n = keep.shape[0] // 2
                send, keep = keep[:n], keep[n:] if n else keep
            results.append(keep[0])
        done.append(jnp.concatenate(results, 0))
    return jnp.concatenate(done, 1)


def solution(mesh):
    n_feat, n_tm = mesh.shape["feat"], mesh.shape["tm"]
    return jax.shard_map(
        functools.partial(shards, n_feat, n_tm),
        mesh=mesh,
        in_specs=(P("tm", "feat"), P("feat", None), P("feat", "tm")),
        out_specs=P(("feat", "tm"), None),
        check_vma=False,
    )
```

```python
import functools

import jax
import jax.numpy as jnp
from jax import lax
from jax.experimental import pallas as pl
from jax.experimental.pallas import tpu as pltpu
from jax.sharding import PartitionSpec as P


PARTS = 2
F32, BF16 = jnp.float32, jnp.bfloat16
VMEM = pl.BlockSpec(memory_space=pltpu.VMEM)
BESIDE = 16
NARROW = 44


def after(x, *earlier):
    return lax.optimization_barrier((x, *earlier))[0]


def swap(x, axis, size, bit):
    return lax.ppermute(x, axis, [(i, i ^ bit) for i in range(size)])


def halves(x):
    hi = x.astype(BF16)
    return hi, (x - hi.astype(F32)).astype(BF16)


def project_kernel(part, other, place, d_ref, e_ref, o_ref):
    _, rows, _ = o_ref.shape
    pair, core = place[1], place[2]
    at = ((core ^ other) * PARTS + part) * 2 * rows
    d = d_ref[pl.ds(pl.multiple_of(at, 2 * rows), 2 * rows), :]
    p = jnp.dot(d, e_ref[...], preferred_element_type=F32)
    for j in range(2):
        o_ref[1 ^ pair ^ j] = p[j * rows : (j + 1) * rows]


def project(dictionary, eigvecs, place, part, other, rows, limit, cost):
    depth, modes = eigvecs.shape
    return pl.pallas_call(
        functools.partial(project_kernel, part, other),
        in_specs=[pl.BlockSpec(memory_space=pltpu.SMEM), VMEM, VMEM],
        out_specs=VMEM,
        out_shape=pltpu.VMEM((2, rows, modes), F32),
        compiler_params=pltpu.CompilerParams(vmem_limit_bytes=limit << 20),
        cost_estimate=pl.CostEstimate(
            flops=4 * rows * depth * modes * cost, bytes_accessed=0, transcendentals=0
        ),
        name="project",
    )(
        place,
        pltpu.with_memory_space_constraint(dictionary, pltpu.VMEM),
        pltpu.with_memory_space_constraint(eigvecs, pltpu.VMEM),
    )


def order(bits):
    if not bits:
        return [0]
    rest = order(bits[1:])
    return [m | bits[0] for m in rest] + rest


def reconstruct_kernel(groups, n_acc, cells, part, place, s_ref, *refs):
    cs, accs = refs[:2], refs[2 : 2 + n_acc]
    outs, both = refs[2 + n_acc : -1], refs[-1]
    _, rows, cols = cs[0].shape
    me, pair, core = place[0], place[1], place[2]
    for i, c in enumerate(cs):
        for j in range(2):
            at = pl.multiple_of((2 * i + (1 ^ pair ^ j)) * rows, rows)
            hi, lo = halves(c[j])
            both[pl.ds(at, rows), :cols] = hi
            both[pl.ds(at, rows), cols:] = lo
    tall = cells // 2
    for g, (p, masks) in enumerate(groups):
        for at, mask in enumerate(masks):
            row = pl.ds(pl.multiple_of((me ^ mask) * cells + p * tall, tall), tall)
            total = accs[g][at] if n_acc else None
            for i in range(2):
                col = ((core ^ 1 ^ i) * PARTS + part) * 2 * rows
                col = pl.ds(pl.multiple_of(col, 2 * rows), 2 * rows)
                hi, lo = halves(s_ref[row, col])
                c = both[2 * i * rows : 2 * (i + 1) * rows, :]
                wide = jnp.dot(hi, c, preferred_element_type=F32)
                low = jnp.dot(lo, c[:, :cols], preferred_element_type=F32)
                term = (wide[:, cols:] + low) + wide[:, :cols]
                total = term if total is None else total + term
            outs[g][at] = total


def reconstruct(snapshots, cs, place, part, groups, cells, accs):
    _, rows, cols = cs[0].shape
    tall = cells // 2
    ins = [pltpu.with_memory_space_constraint(x, pltpu.VMEM) for x in (*cs, *accs)]
    blocks = sum(len(masks) for _, masks in groups)
    return pl.pallas_call(
        functools.partial(reconstruct_kernel, groups, len(accs), cells, part),
        in_specs=[pl.BlockSpec(memory_space=pltpu.SMEM)] + [VMEM] * (1 + len(ins)),
        out_specs=[VMEM] * len(groups),
        scratch_shapes=[pltpu.VMEM((4 * rows, 2 * cols), BF16)],
        out_shape=[pltpu.VMEM((len(masks), tall, cols), F32) for _, masks in groups],
        input_output_aliases={4 + i: i for i in range(len(accs))},
        compiler_params=pltpu.CompilerParams(vmem_limit_bytes=8 << 20),
        cost_estimate=pl.CostEstimate(
            flops=32 * blocks * tall * rows * cols, bytes_accessed=0, transcendentals=0
        ),
        name="reconstruct",
    )(place, snapshots, *ins)


def shards(n_feat, n_tm, dictionary, eigvecs, snapshots):
    feat, tm = lax.axis_index("feat"), lax.axis_index("tm")
    snaps, modes = dictionary.shape[0], eigvecs.shape[1]
    core, pair = feat & 1, (feat >> 1) & 1
    rows = snaps // (4 * PARTS)
    cols = modes // 2
    cells = snapshots.shape[0] // n_tm

    place = jnp.stack([tm, pair, core]).astype(jnp.int32)
    sums, step = [], place
    for part in range(PARTS):
        limit, cost = (NARROW, 1) if part == 0 else (2, BESIDE)
        theirs = project(dictionary, eigvecs, step, part, 1, rows, limit, 1)
        came = swap(theirs, "feat", n_feat, 1)
        step = after(step, theirs)
        mine = project(dictionary, eigvecs, step, part, 0, rows, limit, cost)
        step = after(step, mine)
        sums.append(mine + came)

    streams = [(half, part) for half in range(2) for part in range(PARTS)]
    lag = 2
    totals, full, whole = [], [], []
    for i, (half, part) in enumerate(streams):
        send, keep = (sums[part][j, :, half * cols : (half + 1) * cols] for j in range(2))
        if i >= PARTS:
            keep = after(keep, totals[i - PARTS])
        came = swap(send, "feat", n_feat, 2)
        total = keep + came
        totals.append(total)
        bit = 4
        while bit < n_feat:
            if i >= lag:
                total = after(total, full[i - lag])
            got = swap(total, "feat", n_feat, bit)
            total = total + got
            bit *= 2
        full.append(got)
        other = swap(total, "feat", n_feat, 2)
        own = jnp.stack([other, total])
        whole.append([swap(own, "feat", n_feat, 1), own])

    tm_bits = [1 << i for i in range(n_tm.bit_length() - 1)]
    bit_orders = (tm_bits, tm_bits[::-1])
    sends, keeps = [], []
    for p, bits in enumerate(bit_orders):
        masks = order(bits)
        sends.append((p, masks[: n_tm // 2]))
        keeps.append((p, masks[n_tm // 2 :]))
    done = []
    for half in range(2):
        accs = []
        for part in range(PARTS):
            cs = whole[half * PARTS + part]
            if half == 1 and part == PARTS - 1:
                send = reconstruct(snapshots, cs, place, part, sends, cells, accs[:2])
                keep = reconstruct(snapshots, cs, place, part, keeps, cells, accs[2:])
                accs = send + keep
            else:
                accs = reconstruct(snapshots, cs, place, part, sends + keeps, cells, accs)
        results = []
        for p, bits in enumerate(bit_orders):
            send, keep = accs[p], accs[2 + p]
            for bit in bits:
                keep = keep + swap(send, "tm", n_tm, bit)
                n = keep.shape[0] // 2
                send, keep = keep[:n], keep[n:] if n else keep
            results.append(keep[0])
        done.append(jnp.concatenate(results, 0))
    return jnp.concatenate(done, 1)


def solution(mesh):
    n_feat, n_tm = mesh.shape["feat"], mesh.shape["tm"]

    def body(*args):
        return shards(n_feat, n_tm, *args)

    return jax.shard_map(
        body,
        mesh=mesh,
        in_specs=(P("tm", "feat"), P("feat", None), P("feat", "tm")),
        out_specs=P(("feat", "tm"), None),
        check_vma=False,
    )
```

```python
import functools

import jax
import jax.numpy as jnp
from jax import lax
from jax.experimental import pallas as pl
from jax.experimental.pallas import tpu as pltpu
from jax.sharding import PartitionSpec as P


PARTS = 2
F32, BF16 = jnp.float32, jnp.bfloat16
VMEM = pl.BlockSpec(memory_space=pltpu.VMEM)
BESIDE = 16
NARROW = 44


def after(x, *earlier):
    return lax.optimization_barrier((x, *earlier))[0]


def swap(x, axis, size, bit):
    return lax.ppermute(x, axis, [(i, i ^ bit) for i in range(size)])


def halves(x):
    hi = x.astype(BF16)
    return hi, (x - hi.astype(F32)).astype(BF16)


def position():
    feat = lax.axis_index("feat")
    return lax.axis_index("tm"), (feat >> 1) & 1, feat & 1


def snap_rows(core, other, part, rows):
    at = ((core ^ other) * PARTS + part) * 2 * rows
    return pl.ds(pl.multiple_of(at, 2 * rows), 2 * rows)


def put_projection(d, e, o_ref):
    rows = o_ref.shape[1]
    _, pair, _ = position()
    p = jnp.dot(d, e, preferred_element_type=F32)
    for j in range(2):
        o_ref[1 ^ pair ^ j] = p[j * rows : (j + 1) * rows]


def head_kernel(d_hbm, e_hbm, theirs, mine, d_ref, e_ref, sems):
    rows = theirs.shape[1]
    _, _, core = position()
    e_copy = pltpu.make_async_copy(e_hbm, e_ref, sems.at[0])
    e_copy.start()
    copies = []
    for i in range(2 * PARTS):
        at = snap_rows(core, 1 - i % 2, i // 2, rows)
        copies.append(pltpu.make_async_copy(d_hbm.at[at, :], d_ref.at[at, :], sems.at[1 + i]))
        copies[i].start()
    e_copy.wait()
    for other, o_ref in ((1, theirs), (0, mine)):
        copies[1 - other].wait()
        d = d_ref[snap_rows(core, other, 0, rows), :]
        put_projection(d, e_ref[...], o_ref)
    for copy in copies[2:]:
        copy.wait()


def head(dictionary, eigvecs, rows):
    depth, modes = eigvecs.shape
    hbm = pl.BlockSpec(memory_space=pl.ANY)
    block = pltpu.VMEM((2, rows, modes), F32)
    return pl.pallas_call(
        head_kernel,
        in_specs=[hbm, hbm],
        out_specs=[VMEM] * 4,
        out_shape=[block, block]
        + [pltpu.VMEM(x.shape, x.dtype) for x in (dictionary, eigvecs)],
        scratch_shapes=[pltpu.SemaphoreType.DMA((1 + 2 * PARTS,))],
        compiler_params=pltpu.CompilerParams(vmem_limit_bytes=NARROW << 20),
        cost_estimate=pl.CostEstimate(
            flops=8 * rows * depth * modes,
            bytes_accessed=2 * dictionary.size,
            transcendentals=0,
        ),
        name="head",
    )(*(pltpu.with_memory_space_constraint(x, pltpu.HBM) for x in (dictionary, eigvecs)))


def project_kernel(part, other, order, d_ref, e_ref, o_ref):
    _, _, core = position()
    d = d_ref[snap_rows(core, other, part, o_ref.shape[1]), :]
    put_projection(d, e_ref[...], o_ref)


def project(dictionary, eigvecs, earlier, part, other, rows, cost):
    depth, modes = eigvecs.shape
    return pl.pallas_call(
        functools.partial(project_kernel, part, other),
        in_specs=[pl.BlockSpec(memory_space=pl.ANY), VMEM, VMEM],
        out_specs=VMEM,
        out_shape=pltpu.VMEM((2, rows, modes), F32),
        compiler_params=pltpu.CompilerParams(vmem_limit_bytes=2 << 20),
        cost_estimate=pl.CostEstimate(
            flops=4 * rows * depth * modes * cost, bytes_accessed=0, transcendentals=0
        ),
        name="project",
    )(earlier, dictionary, eigvecs)


def order(bits):
    if not bits:
        return [0]
    rest = order(bits[1:])
    return [m | bits[0] for m in rest] + rest


def reconstruct_kernel(groups, n_acc, cells, part, s_ref, *refs):
    cs, accs = refs[:2], refs[2 : 2 + n_acc]
    outs, both = refs[2 + n_acc : -1], refs[-1]
    _, rows, cols = cs[0].shape
    me, pair, core = position()
    for i, c in enumerate(cs):
        for j in range(2):
            at = pl.multiple_of((2 * i + (1 ^ pair ^ j)) * rows, rows)
            hi, lo = halves(c[j])
            both[pl.ds(at, rows), :cols] = hi
            both[pl.ds(at, rows), cols:] = lo
    tall = cells // 2
    for g, (p, masks) in enumerate(groups):
        for at, mask in enumerate(masks):
            row = pl.ds(pl.multiple_of((me ^ mask) * cells + p * tall, tall), tall)
            total = accs[g][at] if n_acc else None
            for i in range(2):
                hi, lo = halves(s_ref[row, snap_rows(core, 1 - i, part, rows)])
                c = both[2 * i * rows : 2 * (i + 1) * rows, :]
                wide = jnp.dot(hi, c, preferred_element_type=F32)
                low = jnp.dot(lo, c[:, :cols], preferred_element_type=F32)
                term = (wide[:, cols:] + low) + wide[:, :cols]
                total = term if total is None else total + term
            outs[g][at] = total


def reconstruct(snapshots, cs, part, groups, cells, accs):
    _, rows, cols = cs[0].shape
    tall = cells // 2
    ins = [pltpu.with_memory_space_constraint(x, pltpu.VMEM) for x in (*cs, *accs)]
    blocks = sum(len(masks) for _, masks in groups)
    return pl.pallas_call(
        functools.partial(reconstruct_kernel, groups, len(accs), cells, part),
        in_specs=[VMEM] * (1 + len(ins)),
        out_specs=[VMEM] * len(groups),
        scratch_shapes=[pltpu.VMEM((4 * rows, 2 * cols), BF16)],
        out_shape=[pltpu.VMEM((len(masks), tall, cols), F32) for _, masks in groups],
        input_output_aliases={3 + i: i for i in range(len(accs))},
        compiler_params=pltpu.CompilerParams(vmem_limit_bytes=8 << 20),
        cost_estimate=pl.CostEstimate(
            flops=32 * blocks * tall * rows * cols, bytes_accessed=0, transcendentals=0
        ),
        name="reconstruct",
    )(snapshots, *ins)


def shards(n_feat, n_tm, dictionary, eigvecs, snapshots):
    snaps, modes = dictionary.shape[0], eigvecs.shape[1]
    rows = snaps // (4 * PARTS)
    cols = modes // 2
    cells = snapshots.shape[0] // n_tm

    sums = []
    for part in range(PARTS):
        if part == 0:
            theirs, mine, dictionary, eigvecs = head(dictionary, eigvecs, rows)
        else:
            theirs = project(dictionary, eigvecs, mine, part, 1, rows, 1)
        came = swap(theirs, "feat", n_feat, 1)
        if part:
            mine = project(dictionary, eigvecs, theirs, part, 0, rows, BESIDE)
        sums.append(mine + came)

    streams = [(half, part) for half in range(2) for part in range(PARTS)]
    lag = 2
    totals, full, whole = [], [], []
    for i, (half, part) in enumerate(streams):
        send, keep = (sums[part][j, :, half * cols : (half + 1) * cols] for j in range(2))
        if i >= PARTS:
            keep = after(keep, totals[i - PARTS])
        came = swap(send, "feat", n_feat, 2)
        total = keep + came
        totals.append(total)
        bit = 4
        while bit < n_feat:
            if i >= lag:
                total = after(total, full[i - lag])
            got = swap(total, "feat", n_feat, bit)
            total = total + got
            bit *= 2
        full.append(got)
        other = swap(total, "feat", n_feat, 2)
        own = jnp.stack([other, total])
        whole.append([swap(own, "feat", n_feat, 1), own])

    tm_bits = [1 << i for i in range(n_tm.bit_length() - 1)]
    bit_orders = (tm_bits, tm_bits[::-1])
    sends, keeps = [], []
    for p, bits in enumerate(bit_orders):
        masks = order(bits)
        sends.append((p, masks[: n_tm // 2]))
        keeps.append((p, masks[n_tm // 2 :]))
    done = []
    for half in range(2):
        accs = []
        for part in range(PARTS):
            cs = whole[half * PARTS + part]
            if half == 1 and part == PARTS - 1:
                send = reconstruct(snapshots, cs, part, sends, cells, accs[:2])
                keep = reconstruct(snapshots, cs, part, keeps, cells, accs[2:])
                accs = send + keep
            else:
                accs = reconstruct(snapshots, cs, part, sends + keeps, cells, accs)
        results = []
        for p, bits in enumerate(bit_orders):
            send, keep = accs[p], accs[2 + p]
            for bit in bits:
                keep = keep + swap(send, "tm", n_tm, bit)
                n = keep.shape[0] // 2
                send, keep = keep[:n], keep[n:] if n else keep
            results.append(keep[0])
        done.append(jnp.concatenate(results, 0))
    return jnp.concatenate(done, 1)


def solution(mesh):
    n_feat, n_tm = mesh.shape["feat"], mesh.shape["tm"]

    def body(*args):
        return shards(n_feat, n_tm, *args)

    return jax.shard_map(
        body,
        mesh=mesh,
        in_specs=(P("tm", "feat"), P("feat", None), P("feat", "tm")),
        out_specs=P(("feat", "tm"), None),
        check_vma=False,
    )
```

```python
import functools

import jax
import jax.numpy as jnp
from jax import lax
from jax.experimental import pallas as pl
from jax.experimental.pallas import tpu as pltpu
from jax.sharding import PartitionSpec as P


PARTS = 2
STREAMS = ((0, (0,)), (0, (1,)), (1, (0,)), (1, (1,)))
F32, BF16 = jnp.float32, jnp.bfloat16
VMEM = pl.BlockSpec(memory_space=pltpu.VMEM)
BESIDE = 16
NARROW = 44


def after(x, *earlier):
    return lax.optimization_barrier((x, *earlier))[0]


def swap(x, axis, size, bit):
    return lax.ppermute(x, axis, [(i, i ^ bit) for i in range(size)])


def halves(x):
    hi = x.astype(BF16)
    return hi, (x - hi.astype(F32)).astype(BF16)


def position():
    feat = lax.axis_index("feat")
    return lax.axis_index("tm"), (feat >> 1) & 1, feat & 1


def snap_rows(core, other, part, rows):
    at = ((core ^ other) * PARTS + part) * 2 * rows
    return pl.ds(pl.multiple_of(at, 2 * rows), 2 * rows)


def put_projection(d, e, o_ref):
    rows = o_ref.shape[1]
    _, pair, _ = position()
    p = jnp.dot(d, e, preferred_element_type=F32)
    for j in range(2):
        o_ref[1 ^ pair ^ j] = p[j * rows : (j + 1) * rows]


def head_kernel(d_hbm, e_hbm, theirs, mine, d_ref, e_ref, sems):
    rows = theirs.shape[1]
    _, _, core = position()
    e_copy = pltpu.make_async_copy(e_hbm, e_ref, sems.at[0])
    e_copy.start()
    copies = []
    for i in range(2 * PARTS):
        at = snap_rows(core, 1 - i % 2, i // 2, rows)
        copies.append(pltpu.make_async_copy(d_hbm.at[at, :], d_ref.at[at, :], sems.at[1 + i]))
        copies[i].start()
    e_copy.wait()
    for other, o_ref in ((1, theirs), (0, mine)):
        copies[1 - other].wait()
        d = d_ref[snap_rows(core, other, 0, rows), :]
        put_projection(d, e_ref[...], o_ref)
    for copy in copies[2:]:
        copy.wait()


def head(dictionary, eigvecs, rows):
    depth, modes = eigvecs.shape
    hbm = pl.BlockSpec(memory_space=pl.ANY)
    block = pltpu.VMEM((2, rows, modes), F32)
    return pl.pallas_call(
        head_kernel,
        in_specs=[hbm, hbm],
        out_specs=[VMEM] * 4,
        out_shape=[block, block]
        + [pltpu.VMEM(x.shape, x.dtype) for x in (dictionary, eigvecs)],
        scratch_shapes=[pltpu.SemaphoreType.DMA((1 + 2 * PARTS,))],
        compiler_params=pltpu.CompilerParams(vmem_limit_bytes=NARROW << 20),
        cost_estimate=pl.CostEstimate(
            flops=8 * rows * depth * modes,
            bytes_accessed=2 * dictionary.size,
            transcendentals=0,
        ),
        name="head",
    )(*(pltpu.with_memory_space_constraint(x, pltpu.HBM) for x in (dictionary, eigvecs)))


def project_kernel(part, other, order, d_ref, e_ref, o_ref):
    _, _, core = position()
    d = d_ref[snap_rows(core, other, part, o_ref.shape[1]), :]
    put_projection(d, e_ref[...], o_ref)


def project(dictionary, eigvecs, earlier, part, other, rows, cost):
    depth, modes = eigvecs.shape
    return pl.pallas_call(
        functools.partial(project_kernel, part, other),
        in_specs=[pl.BlockSpec(memory_space=pl.ANY), VMEM, VMEM],
        out_specs=VMEM,
        out_shape=pltpu.VMEM((2, rows, modes), F32),
        compiler_params=pltpu.CompilerParams(vmem_limit_bytes=2 << 20),
        cost_estimate=pl.CostEstimate(
            flops=4 * rows * depth * modes * cost, bytes_accessed=0, transcendentals=0
        ),
        name="project",
    )(earlier, dictionary, eigvecs)


def order(bits):
    if not bits:
        return [0]
    rest = order(bits[1:])
    return [m | bits[0] for m in rest] + rest


def reconstruct_kernel(groups, n_acc, cells, parts, s_ref, *refs):
    cs, accs = refs[:2], refs[2 : 2 + n_acc]
    outs, both = refs[2 + n_acc : -1], refs[-1]
    _, rows, cols = cs[0].shape
    rows //= len(parts)
    me, pair, core = position()
    pieces = [(i, k) for i in range(2) for k in range(len(parts))]
    for n, (i, k) in enumerate(pieces):
        for j in range(2):
            at = pl.multiple_of((2 * n + (1 ^ pair ^ j)) * rows, rows)
            hi, lo = halves(cs[i][j, k * rows : (k + 1) * rows])
            both[pl.ds(at, rows), :cols] = hi
            both[pl.ds(at, rows), cols:] = lo
    tall = cells // 2
    for g, (p, masks) in enumerate(groups):
        for at, mask in enumerate(masks):
            row = pl.ds(pl.multiple_of((me ^ mask) * cells + p * tall, tall), tall)
            total = accs[g][at] if n_acc else None
            for n, (i, k) in enumerate(pieces):
                hi, lo = halves(s_ref[row, snap_rows(core, 1 - i, parts[k], rows)])
                c = both[2 * n * rows : 2 * (n + 1) * rows, :]
                wide = jnp.dot(hi, c, preferred_element_type=F32)
                low = jnp.dot(lo, c[:, :cols], preferred_element_type=F32)
                term = (wide[:, cols:] + low) + wide[:, :cols]
                total = term if total is None else total + term
            outs[g][at] = total


def reconstruct(snapshots, cs, parts, groups, cells, accs):
    _, rows, cols = cs[0].shape
    tall = cells // 2
    ins = [pltpu.with_memory_space_constraint(x, pltpu.VMEM) for x in (*cs, *accs)]
    blocks = sum(len(masks) for _, masks in groups)
    return pl.pallas_call(
        functools.partial(reconstruct_kernel, groups, len(accs), cells, parts),
        in_specs=[VMEM] * (1 + len(ins)),
        out_specs=[VMEM] * len(groups),
        scratch_shapes=[pltpu.VMEM((4 * rows, 2 * cols), BF16)],
        out_shape=[pltpu.VMEM((len(masks), tall, cols), F32) for _, masks in groups],
        input_output_aliases={3 + i: i for i in range(len(accs))},
        compiler_params=pltpu.CompilerParams(vmem_limit_bytes=8 << 20),
        cost_estimate=pl.CostEstimate(
            flops=32 * blocks * tall * rows * cols, bytes_accessed=0, transcendentals=0
        ),
        name="reconstruct",
    )(snapshots, *ins)


def shards(n_feat, n_tm, dictionary, eigvecs, snapshots):
    snaps, modes = dictionary.shape[0], eigvecs.shape[1]
    rows = snaps // (4 * PARTS)
    cols = modes // 2
    cells = snapshots.shape[0] // n_tm

    sums = []
    for part in range(PARTS):
        if part == 0:
            theirs, mine, dictionary, eigvecs = head(dictionary, eigvecs, rows)
        else:
            theirs = project(dictionary, eigvecs, mine, part, 1, rows, 1)
        came = swap(theirs, "feat", n_feat, 1)
        if part:
            mine = project(dictionary, eigvecs, theirs, part, 0, rows, BESIDE)
        sums.append(mine + came)

    lag = 2
    totals, full, whole = [], [], [[], []]
    for i, (half, parts) in enumerate(STREAMS):
        at = slice(half * cols, (half + 1) * cols)
        send, keep = (
            jnp.concatenate([sums[part][j, :, at] for part in parts]) for j in range(2)
        )
        if half:
            keep = after(keep, totals[0])
        came = swap(send, "feat", n_feat, 2)
        total = keep + came
        totals.append(total)
        bit = 4
        while bit < n_feat:
            if i >= lag:
                total = after(total, full[i - lag])
            got = swap(total, "feat", n_feat, bit)
            total = total + got
            bit *= 2
        full.append(got)
        other = swap(total, "feat", n_feat, 2)
        own = jnp.stack([other, total])
        whole[half].append(([swap(own, "feat", n_feat, 1), own], parts))

    tm_bits = [1 << i for i in range(n_tm.bit_length() - 1)]
    bit_orders = (tm_bits, tm_bits[::-1])
    sends, keeps = [], []
    for p, bits in enumerate(bit_orders):
        masks = order(bits)
        sends.append((p, masks[: n_tm // 2]))
        keeps.append((p, masks[n_tm // 2 :]))
    done = []
    for half in range(2):
        accs = []
        for n, (cs, parts) in enumerate(whole[half]):
            if half == 1 and n == len(whole[half]) - 1:
                send = reconstruct(snapshots, cs, parts, sends, cells, accs[:2])
                keep = reconstruct(snapshots, cs, parts, keeps, cells, accs[2:])
                accs = send + keep
            else:
                accs = reconstruct(snapshots, cs, parts, sends + keeps, cells, accs)
        results = []
        for p, bits in enumerate(bit_orders):
            send, keep = accs[p], accs[2 + p]
            for bit in bits:
                keep = keep + swap(send, "tm", n_tm, bit)
                n = keep.shape[0] // 2
                send, keep = keep[:n], keep[n:] if n else keep
            results.append(keep[0])
        done.append(jnp.concatenate(results, 0))
    return jnp.concatenate(done, 1)


def solution(mesh):
    n_feat, n_tm = mesh.shape["feat"], mesh.shape["tm"]

    def body(*args):
        return shards(n_feat, n_tm, *args)

    return jax.shard_map(
        body,
        mesh=mesh,
        in_specs=(P("tm", "feat"), P("feat", None), P("feat", "tm")),
        out_specs=P(("feat", "tm"), None),
        check_vma=False,
    )
```
